128 devices in a mesh: dp: 4 (over x_lo, core), tensor: 32 (over y, x_hi, z).
Axes of the slice: x: 4 (x_hi: 2, x_lo: 2; x = x_hi * 2 + x_lo), y: 4, z: 4, core: 2. Of those that a mesh axis runs over, the one named last changes fastest.
Arguments:
- qkv_master: float32 [7168, 21504], P(('dp', 'tensor')), may hold values from -0.0625 to 0.0625
- adapter_down: float32 [13, 7168, 128], P(None, ('dp', 'tensor')), may hold values from -0.0625 to 0.0625
- adapter_up: float32 [13, 128, 21504], P(None, None, 'tensor'), may hold values from -0.5 to 0.5
- adapter_pick: int32 [1], replicated, may hold values from 0 to 12
- out_master: float32 [3584, 7168], P(('dp', 'tensor')), may hold values from -0.0625 to 0.0625
- norm_gain: float32 [7168], replicated, may hold values from 0.1 to 1.9
- hidden_in: bfloat16 [2048, 3584], P(('dp', 'tensor')), may hold values from -6 to 6
- embed_in: bfloat16 [2048, 3584], P(('dp', 'tensor')), may hold values from -6 to 6
- prompt_len: int32 [4, 2], P('dp'), may hold values from 1 to 511, as said below
- prefix_len: int32 [4, 2], P('dp'), may hold values from 0 to 512, as said below
- prefix_holder: int32 [4, 2], P('dp'), may hold values from 0 to 3
- prefix_keys: bfloat16 [4, 512, 7168], P('dp', None, 'tensor'), may hold values from -6 to 6
- prefix_values: bfloat16 [4, 512, 7168], P('dp', None, 'tensor'), may hold values from -6 to 6
Outputs:
- server_qkv: bfloat16 [7168, 21504], P(None, 'tensor')
- server_out: bfloat16 [3584, 7168], P(None, 'tensor')
- block_out: bfloat16 [2048, 3584], P(('dp', 'tensor'))
- new_keys: bfloat16 [2048, 7168], P('dp', 'tensor')
- new_values: bfloat16 [2048, 7168], P('dp', 'tensor')
The draws below stay inside these ranges and needn't reach their ends.
Inputs may be any that keep to these rules, and one draw needn't show every extreme that they name: `prompt_len`: the two prompt lengths of a replica add up to 512. `prefix_len`: exactly half of all requests extend a cached prefix (a positive length); the others have 0.
All inputs are finite; a program needn't handle non-finite values.
Results may differ from the reference program's by a relative error of at most 0.033.
Values may be sent and summed in bfloat16 or wider, within the bound.
A program may use at most 128 MiB of HBM per device.

```python
import math
import jax
import jax.numpy as jnp
from jax import lax

D_MODEL = 3584
D_IN = 7168
HD = 224
HEADS = 32
RANK = 128
ADAPTERS = 13
TOK_REP = 512
TOKENS = 2048
PREF_MAX = 512
QKV = 21504
ATT = 7168
N_DP = 4


def draw_prompt_len(key, part):
    key_first, key_full = jax.random.split(key)
    first_len = jax.random.randint(key_first, (N_DP,), 1, TOK_REP)
    full_replica = jax.random.randint(key_full, (), 0, N_DP)
    first_len = jnp.where(jnp.arange(N_DP) == full_replica, TOK_REP - 1, first_len)
    return jnp.stack([first_len, TOK_REP - first_len], axis=1).astype(jnp.int32)


def draw_prefix_len(key, part):
    key_order, key_len = jax.random.split(key)
    ordering = jax.random.permutation(key_order, 2 * N_DP)
    lengths = jax.random.randint(key_len, (2 * N_DP,), 1, PREF_MAX + 1)
    lengths = lengths.at[ordering[0]].set(PREF_MAX)
    chosen = jnp.zeros((2 * N_DP,), jnp.int32).at[ordering[:N_DP]].set(1)
    return (lengths * chosen).reshape(N_DP, 2).astype(jnp.int32)


def set_ends(array, stream_key, smallest, high):
    index_at = [jax.random.randint(jax.random.fold_in(stream_key, axis), (), 0, length) for axis, length in enumerate(array.shape)]
    longest = array.shape.index(max(array.shape))
    beside = index_at[:longest] + [(index_at[longest] + 1) % array.shape[longest]] + index_at[longest + 1:]
    return array.at[tuple(index_at)].set(smallest).at[tuple(beside)].set(high)


def steps_of(key, dims, shards, low, largest):
    factor_of = 1.0
    for axis_at, parts in shards:
        heights = jax.random.uniform(jax.random.fold_in(jax.random.fold_in(key, 6), axis_at), (parts,), jnp.float32, low / len(shards), largest / len(shards))
        factor_of = factor_of * jnp.repeat(jnp.exp(heights), dims[axis_at] // parts).reshape((-1,) + (1,) * (len(dims) - 1 - axis_at))
    return factor_of


def scatter_about(rng, dims, deviation, reach, cuts=(), held_as=jnp.bfloat16):
    entries = deviation * jax.random.normal(rng, dims, jnp.float32)
    if cuts:
        entries = entries * steps_of(rng, dims, cuts, -0.22, 0.18)
    return jnp.clip(entries, -reach, reach).astype(held_as)


def setup_inputs(seed: int = 0) -> dict:
    keys = jax.random.split(jax.random.key(seed), 14)
    return {
        "qkv_master": scatter_about(keys[0], (D_IN, QKV), D_IN ** -0.5, 0.0625, ((0, 128),), jnp.float32),
        "adapter_down": scatter_about(keys[1], (ADAPTERS, D_IN, RANK), D_IN ** -0.5, 0.0625, ((1, 128),), jnp.float32),
        "adapter_up": scatter_about(keys[2], (ADAPTERS, RANK, QKV), RANK ** -0.5, 0.5, ((2, 32),), jnp.float32),
        "adapter_pick": jax.random.randint(keys[3], (1,), 0, ADAPTERS).astype(jnp.int32),
        "out_master": scatter_about(keys[4], (D_MODEL, ATT), ATT ** -0.5, 0.0625, ((0, 128),), jnp.float32),
        "norm_gain": jnp.clip(1.0 + 0.18 * jax.random.normal(keys[5], (D_IN,), jnp.float32), 0.1, 1.9),
        "hidden_in": scatter_about(keys[6], (TOKENS, D_MODEL), 1.0, 6.0, ((0, 128),)),
        "embed_in": scatter_about(keys[7], (TOKENS, D_MODEL), 1.0, 6.0, ((0, 128),)),
        "prompt_len": draw_prompt_len(jax.random.fold_in(keys[13], 71), 0),
        "prefix_len": draw_prefix_len(jax.random.fold_in(keys[13], 71), 0),
        "prefix_holder": set_ends(jax.random.randint(keys[10], (N_DP, 2), 0, N_DP), jax.random.fold_in(keys[10], 1), 0, N_DP - 1).astype(jnp.int32),
        "prefix_keys": scatter_about(keys[11], (N_DP, PREF_MAX, ATT), 1.0, 6.0, ((0, 4), (2, 32))),
        "prefix_values": scatter_about(keys[12], (N_DP, PREF_MAX, ATT), 1.0, 6.0, ((0, 4), (2, 32))),
    }


def replica_attention(head_qkv, lengths, cached_len, holders, prefix_keys, prefix_values):
    as_float = head_qkv.astype(jnp.float32)
    queries = as_float[:, :, 0]
    key_rows = as_float[:, :, 1]
    value_rows = as_float[:, :, 2]
    inv_scale = 1.0 / math.sqrt(HD)
    positions = jnp.arange(TOK_REP, dtype=jnp.int32)
    request = (positions >= lengths[0]).astype(jnp.int32)
    allowed = (request[:, None] == request[None, :]) & (positions[None, :] <= positions[:, None])
    scores = jnp.einsum('qhd,khd->hqk', queries, key_rows) * inv_scale
    weights = jnp.where(allowed[None], jnp.exp(scores), jnp.float32(0.0))
    weight_sum = lax.optimization_barrier(jnp.sum(weights, axis=2))
    rounded = lax.optimization_barrier(weights.astype(jnp.bfloat16)).astype(jnp.float32)
    numerator = jnp.einsum('hqk,khd->hqd', rounded, value_rows)
    slot_ids = jnp.arange(PREF_MAX, dtype=jnp.int32)
    for member in range(2):
        cached_keys = lax.dynamic_index_in_dim(prefix_keys, holders[member], 0, keepdims=False)
        cached_keys = cached_keys.reshape(PREF_MAX, HEADS, HD).astype(jnp.float32)
        cached_values = lax.dynamic_index_in_dim(prefix_values, holders[member], 0, keepdims=False)
        cached_values = cached_values.reshape(PREF_MAX, HEADS, HD).astype(jnp.float32)
        usable = (request == member)[:, None] & (slot_ids[None, :] < cached_len[member])
        scores = jnp.einsum('qhd,khd->hqk', queries, cached_keys) * inv_scale
        weights = jnp.where(usable[None], jnp.exp(scores), jnp.float32(0.0))
        weight_sum = weight_sum + lax.optimization_barrier(jnp.sum(weights, axis=2))
        rounded = lax.optimization_barrier(weights.astype(jnp.bfloat16)).astype(jnp.float32)
        numerator = numerator + jnp.einsum('hqk,khd->hqd', rounded, cached_values)
    attended = numerator / weight_sum[:, :, None]
    return jnp.transpose(attended, (1, 0, 2)).reshape(TOK_REP, HEADS * HD).astype(jnp.bfloat16)

def reference(qkv_master, adapter_down, adapter_up, adapter_pick, out_master, norm_gain, hidden_in, embed_in, prompt_len, prefix_len, prefix_holder, prefix_keys, prefix_values):
    chosen = adapter_pick[0]
    down_pick = lax.dynamic_index_in_dim(adapter_down, chosen, 0, keepdims=False).astype(jnp.bfloat16)
    up_pick = lax.dynamic_index_in_dim(adapter_up, chosen, 0, keepdims=False).astype(jnp.bfloat16)
    server_qkv = (qkv_master + jnp.dot(down_pick, up_pick, preferred_element_type=jnp.float32)).astype(jnp.bfloat16)
    server_out = out_master.astype(jnp.bfloat16)
    joined = jnp.concatenate([hidden_in, embed_in], axis=1).astype(jnp.float32)
    factor = lax.rsqrt(lax.optimization_barrier(jnp.mean(joined * joined, axis=1, keepdims=True)) + 1e-05)
    normed = (joined * factor * norm_gain).astype(jnp.bfloat16)
    qkv_all = jnp.dot(normed, server_qkv, preferred_element_type=jnp.float32).astype(jnp.bfloat16)
    qkv_all = lax.optimization_barrier(qkv_all)
    grouped = qkv_all.reshape(TOKENS, HEADS, 3, HD)
    new_keys = grouped[:, :, 1].reshape(TOKENS, HEADS * HD)
    new_values = grouped[:, :, 2].reshape(TOKENS, HEADS * HD)
    attended = []
    for replica in range(N_DP):
        head_qkv = grouped[replica * TOK_REP:(replica + 1) * TOK_REP]
        attended.append(replica_attention(head_qkv, prompt_len[replica], prefix_len[replica], prefix_holder[replica], prefix_keys, prefix_values))
    attention = jnp.concatenate(attended, axis=0)
    block_out = lax.dot_general(attention, server_out, (((1,), (1,)), ((), ())), preferred_element_type=jnp.float32).astype(jnp.bfloat16)
    return (server_qkv, server_out, block_out, new_keys, new_values)
```

```python
import functools
import math

import jax
import jax.numpy as jnp
from jax import lax
from jax.experimental import pallas as pl
from jax.experimental.pallas import tpu as pltpu
from jax.sharding import PartitionSpec as P

MESH = pl.DeviceIdType.MESH
N_Y, N_XH, N_Z = 4, 2, 4


def position():
    dp = lax.axis_index("dp")
    t = lax.axis_index("tensor")
    xl, c = lax.div(dp, 2), lax.rem(dp, 2)
    y, xh, z = lax.div(t, 8), lax.rem(lax.div(t, 4), 2), lax.rem(t, 4)
    return dp, t, xl, c, y, xh, z


def tensor_of(y, xh, z):
    return y * 8 + xh * 4 + z


def pack_kernel(master_ref, out_ref, down_ref, a_ref, b_ref):
    rows, width = master_ref.shape
    out_rows, out_width = out_ref.shape
    cols, out_cols = width // 4, out_width // 4
    whole = cols // 128 * 128
    master = master_ref[...].astype(jnp.bfloat16).astype(jnp.float32)
    outs = out_ref[...]
    down = down_ref[...].astype(jnp.bfloat16)
    for k in range(4):
        a_ref[k, :, 0:cols] = master[:, k * cols : (k + 1) * cols].astype(jnp.bfloat16)
        piece = outs[:, k * out_cols : (k + 1) * out_cols]
        a_ref[k, 0:out_rows, cols:768] = piece[:, 128:].astype(jnp.bfloat16)
        a_ref[k, out_rows:, cols:768] = jnp.zeros((rows - out_rows, 768 - cols), jnp.bfloat16)
        b_ref[k, 0:rows, :] = down
        b_ref[k, rows : rows + 32, :] = jnp.concatenate(
            [piece[:, :128], jnp.zeros((32 - out_rows, 128), jnp.float32)], axis=0
        ).astype(jnp.bfloat16)


def pack(master, outs, down):
    rows, out_rows = master.shape[0], outs.shape[0]
    n = 8
    return pl.pallas_call(
        pack_kernel,
        grid=(n,),
        in_specs=[
            pl.BlockSpec((rows, master.shape[1] // n), lambda i: (0, i)),
            pl.BlockSpec((out_rows, outs.shape[1] // n), lambda i: (0, i)),
            pl.BlockSpec(down.shape, lambda i: (0, 0)),
        ],
        out_specs=[
            pl.BlockSpec((4, rows, 768), lambda i: (i, 0, 0)),
            pl.BlockSpec((4, rows + 32, 128), lambda i: (i, 0, 0)),
        ],
        out_shape=[
            jax.ShapeDtypeStruct((32, rows, 768), jnp.bfloat16),
            jax.ShapeDtypeStruct((32, rows + 32, 128), jnp.bfloat16),
        ],
    )(master, outs, down)


def exchange_kernel(
    sa, sb, na, nb, pk, pv,
    ra, rb, xa, xb, gk, gv,
    w_send, w_recv, n_send, n_recv, s_send, s_recv, f_send, f_recv,
    t_send, t_recv, p_send, p_recv, l_sem,
):
    dp, t, xl, c, y, xh, z = position()
    near = (1 - xl) * 2 + c
    core = xl * 2 + (1 - c)
    me = dp * 32 + t

    def remote(src, dst, send, recv, to_dp, to_t):
        return pltpu.make_async_remote_copy(
            src_ref=src, dst_ref=dst, send_sem=send, recv_sem=recv,
            device_id=(to_dp, to_t), device_id_type=MESH,
        )

    own = [
        pltpu.make_async_copy(na, xa.at[y * 2 + xh, z], l_sem.at[0]),
        pltpu.make_async_copy(nb, xb.at[y * 2 + xh, z], l_sem.at[1]),
        pltpu.make_async_copy(sa.at[t], ra.at[me], l_sem.at[2]),
        pltpu.make_async_copy(sb.at[t], rb.at[me], l_sem.at[3]),
        pltpu.make_async_copy(pk, gk.at[dp], l_sem.at[4]),
        pltpu.make_async_copy(pv, gv.at[dp], l_sem.at[5]),
    ]
    for copy in own:
        copy.start()

    other = tensor_of(y, 1 - xh, z)
    step1 = [
        remote(na, xa.at[y * 2 + xh, z], t_send.at[0], t_recv.at[0], dp, other),
        remote(nb, xb.at[y * 2 + xh, z], t_send.at[1], t_recv.at[1], dp, other),
    ]
    for copy in step1:
        copy.start()

    prefix = []
    for i, (src, dst) in enumerate(((pk, gk), (pv, gv))):
        prefix.append(remote(src, dst.at[dp], p_send.at[i], p_recv.at[i], near, t))
        prefix.append(remote(src, dst.at[dp], p_send.at[2 + i], p_recv.at[2 + i], core, t))
    for copy in prefix:
        copy.start()

    def chunk(i, which, sign):
        a, s, b = lax.div(i, 8), lax.rem(lax.div(i, 4), 2), lax.rem(i, 4)
        to_dp = lax.rem(xl + s, 2) * 2 + c
        to_t = tensor_of(lax.rem(y + a, 4), lax.rem(xh + s, 2), lax.rem(z + b, 4))
        src, dst = ((sa, ra), (sb, rb))[which]
        return remote(
            src.at[to_t], dst.at[me], w_send.at[which, i], w_recv.at[which, i], to_dp, to_t
        )

    def send_chunk(i, carry):
        chunk(i, 0, 1).start()
        chunk(i, 1, 1).start()
        return carry

    lax.fori_loop(1, 32, send_chunk, 0)

    for copy in step1:
        copy.wait_recv()
    own[0].wait()
    own[1].wait()
    step2 = []
    for d in range(1, 4):
        to_z = tensor_of(y, xh, lax.rem(z + d, 4))
        to_y = tensor_of(lax.rem(y + d, 4), xh, z)
        mine = pl.ds(y * 2, 2)
        step2.append(
            remote(xa.at[mine, z], xa.at[mine, z], t_send.at[1 + d], t_recv.at[1 + d], dp, to_z)
        )
        step2.append(
            remote(xb.at[mine, z], xb.at[mine, z], t_send.at[4 + d], t_recv.at[4 + d], dp, to_y)
        )
    for copy in step2:
        copy.start()

    own[2].wait()
    own[3].wait()

    def first_of(j, from_xl):
        a, s = lax.div(j, 2), lax.rem(j, 2)
        src_dp = lax.rem(from_xl + s, 2) * 2
        return src_dp * 32 + tensor_of(lax.rem(y + 4 - a, 4), lax.rem(xh + s, 2), 0)

    def group(j, which, send, recv, to_dp, from_xl, from_c):
        g = first_of(j, from_xl) + from_c * 32
        ref = (ra, rb)[which].at[pl.ds(g, 4)]
        return remote(ref, ref, send.at[which, j], recv.at[which, j], to_dp, t)

    def forward(j, carry):
        for which in range(2):
            for b in range(4):
                i = j * 4 + b

                @pl.when(i > 0)
                def _():
                    chunk(i, which, 1).wait_recv()

            group(j, which, n_send, n_recv, near, xl, c).start()
            group(j, which, s_send, s_recv, core, xl, c).start()
        return carry

    lax.fori_loop(0, 4, forward, 0)

    for copy in step2:
        copy.wait_recv()
    step3 = []
    for k, d in enumerate((1, 3)):
        to_y = tensor_of(lax.rem(y + d, 4), xh, z)
        to_z = tensor_of(y, xh, lax.rem(z + d, 4))
        for h in range(2):
            rows = pl.ds(y * 2 + h, 1)
            step3.append(
                remote(
                    xa.at[rows], xa.at[rows],
                    t_send.at[8 + k * 2 + h], t_recv.at[8 + k * 2 + h], dp, to_y,
                )
            )
            rows = pl.ds(h * 4, 4)
            step3.append(
                remote(
                    xb.at[rows, z], xb.at[rows, z],
                    t_send.at[12 + k * 2 + h], t_recv.at[12 + k * 2 + h], dp, to_z,
                )
            )
    for copy in step3:
        copy.start()

    lax.fori_loop(4, 8, forward, 0)

    late = []
    for i, dst in enumerate((gk, gv)):
        prefix[2 * i].wait_recv()
        late.append(
            remote(dst.at[near], dst.at[near], p_send.at[4 + i], p_recv.at[4 + i], core, t)
        )
        late[-1].start()

    for copy in step3:
        copy.wait_recv()
    step4 = []
    for h, d in ((0, 1), (1, 3)):
        src_y, src_z = lax.rem(y + 4 - d, 4), lax.rem(z + 4 - d, 4)
        to_y = tensor_of(lax.rem(y + d, 4), xh, z)
        to_z = tensor_of(y, xh, lax.rem(z + d, 4))
        rows = pl.ds(src_y * 2 + h, 1)
        step4.append(
            remote(xa.at[rows], xa.at[rows], t_send.at[16 + h], t_recv.at[16 + h], dp, to_y)
        )
        rows = pl.ds(h * 4, 4)
        step4.append(
            remote(
                xb.at[rows, src_z], xb.at[rows, src_z],
                t_send.at[18 + h], t_recv.at[18 + h], dp, to_z,
            )
        )
    for copy in step4:
        copy.start()

    def pass_on(j, carry):
        for which in range(2):
            group(j, which, n_send, n_recv, near, xl, c).wait_recv()
            group(j, which, f_send, f_recv, core, 1 - xl, c).start()
        return carry

    lax.fori_loop(0, 8, pass_on, 0)

    def finish(j, carry):
        for which in range(2):
            group(j, which, s_send, s_recv, core, xl, c).wait_recv()
            group(j, which, f_send, f_recv, core, 1 - xl, c).wait()
            group(j, which, n_send, n_recv, near, xl, c).wait_send()
            group(j, which, s_send, s_recv, core, xl, c).wait_send()
        return carry

    lax.fori_loop(0, 8, finish, 0)

    def sent(i, carry):
        chunk(i, 0, 1).wait_send()
        chunk(i, 1, 1).wait_send()
        return carry

    lax.fori_loop(1, 32, sent, 0)
    for copy in step4:
        copy.wait_recv()
    for copy in step1 + step2 + step3 + step4:
        copy.wait_send()
    own[4].wait()
    own[5].wait()
    for i in range(2):
        prefix[2 * i + 1].wait_recv()
    for copy in prefix:
        copy.wait_send()
    for copy in late:
        copy.wait()


def exchange(sa, sb, na, nb, pk, pv):
    half = na.shape[1]
    any_spec = pl.BlockSpec(memory_space=pl.ANY)
    bf16 = jnp.bfloat16
    dma = pltpu.SemaphoreType.DMA
    return pl.pallas_call(
        exchange_kernel,
        in_specs=[any_spec] * 6,
        out_specs=[any_spec] * 6,
        out_shape=[
            jax.ShapeDtypeStruct((128,) + sa.shape[1:], bf16),
            jax.ShapeDtypeStruct((128,) + sb.shape[1:], bf16),
            jax.ShapeDtypeStruct((8, 4, 16, half), bf16),
            jax.ShapeDtypeStruct((8, 4, 16, half), bf16),
            jax.ShapeDtypeStruct((4,) + pk.shape, bf16),
            jax.ShapeDtypeStruct((4,) + pv.shape, bf16),
        ],
        scratch_shapes=[
            dma((2, 32)), dma((2, 32)),
            dma((2, 8)), dma((2, 8)),
            dma((2, 8)), dma((2, 8)),
            dma((2, 8)), dma((2, 8)),
            dma((20,)), dma((20,)),
            dma((6,)), dma((6,)),
            dma((6,)),
        ],
        compiler_params=pltpu.CompilerParams(has_side_effects=True),
        name="exchange",
    )(sa, sb, na, nb, pk, pv)


def project_kernel(
    attn, weights, out,
    pa, pb, ra1, rb1, qa, qb, ra2, rb2, ha, hb, ra3, rb3,
    send, recv,
):
    dp, t, xl, c, y, xh, z = position()
    half = pa.shape[-1]
    step = 256

    def remote(src, dst, k, to_t):
        return pltpu.make_async_remote_copy(
            src_ref=src, dst_ref=dst, send_sem=send.at[k], recv_sem=recv.at[k],
            device_id=(dp, to_t), device_id_type=MESH,
        )

    def fill(dst, first):
        for f in range(half // step):
            block = lax.dot_general(
                attn[...],
                weights[first + f * step : first + (f + 1) * step, :],
                (((1,), (1,)), ((), ())),
                preferred_element_type=jnp.float32,
            )
            dst[:, :, :, f * step : (f + 1) * step] = block.astype(jnp.bfloat16).reshape(
                8, 4, 16, step
            )

    def f32(x):
        return x.astype(jnp.float32)

    fill(pa, 0)
    a1, b1, a2, b2 = [], [], [], []
    for d in range(1, 4):
        to = lax.rem(z + d, 4)
        a1.append(remote(pa.at[:, to], ra1.at[d - 1], d - 1, tensor_of(y, xh, to)))
        a1[-1].start()
    fill(pb, half)
    for d in range(1, 4):
        to = lax.rem(y + d, 4)
        b1.append(remote(pb.at[pl.ds(to * 2, 2)], rb1.at[d - 1], 2 + d, tensor_of(to, xh, z)))
        b1[-1].start()

    for copy in a1:
        copy.wait_recv()
    for i in range(8):
        total = f32(pa[i, z]) + f32(ra1[0, i]) + f32(ra1[1, i]) + f32(ra1[2, i])
        qa[i] = total.astype(jnp.bfloat16)
    for d in range(1, 4):
        to = lax.rem(y + d, 4)
        a2.append(remote(qa.at[pl.ds(to * 2, 2)], ra2.at[d - 1], 5 + d, tensor_of(to, xh, z)))
        a2[-1].start()
    for copy in b1:
        copy.wait_recv()
    for h in range(2):
        for i in range(4):
            total = f32(pb[y * 2 + h, i]) + f32(rb1[0, h, i]) + f32(rb1[1, h, i])
            qb[h, i] = (total + f32(rb1[2, h, i])).astype(jnp.bfloat16)
    for d in range(1, 4):
        to = lax.rem(z + d, 4)
        b2.append(remote(qb.at[:, to], rb2.at[d - 1], 8 + d, tensor_of(y, xh, to)))
        b2[-1].start()

    partner = tensor_of(y, 1 - xh, z)
    for copy in a2:
        copy.wait_recv()
    for h in range(2):
        total = f32(qa[y * 2 + h]) + f32(ra2[0, h]) + f32(ra2[1, h]) + f32(ra2[2, h])
        ha[h] = total.astype(jnp.bfloat16)
    a3 = remote(ha.at[1 - xh], ra3, 12, partner)
    a3.start()
    for copy in b2:
        copy.wait_recv()
    for h in range(2):
        total = f32(qb[h, z]) + f32(rb2[0, h]) + f32(rb2[1, h]) + f32(rb2[2, h])
        hb[h] = total.astype(jnp.bfloat16)
    b3 = remote(hb.at[1 - xh], rb3, 13, partner)
    b3.start()
    a3.wait_recv()
    out[:, :half] = (f32(ha[xh]) + f32(ra3[...])).astype(jnp.bfloat16)
    b3.wait_recv()
    out[:, half:] = (f32(hb[xh]) + f32(rb3[...])).astype(jnp.bfloat16)
    for copy in a1 + b1 + a2 + b2 + [a3, b3]:
        copy.wait_send()


def project(attn, weights):
    features = weights.shape[0]
    half = features // 2
    vmem = pl.BlockSpec(memory_space=pltpu.VMEM)

    def room(*shape):
        return pltpu.VMEM(shape + (16, half), jnp.bfloat16)

    return pl.pallas_call(
        project_kernel,
        in_specs=[vmem] * 2,
        out_specs=vmem,
        out_shape=jax.ShapeDtypeStruct((16, features), jnp.bfloat16),
        scratch_shapes=[
            room(8, 4), room(8, 4),
            room(3, 8), room(3, 2, 4),
            room(8), room(2, 4),
            room(3, 2), room(3, 2),
            room(2), room(2),
            room(), room(),
            pltpu.SemaphoreType.DMA((14,)),
            pltpu.SemaphoreType.DMA((14,)),
        ],
        compiler_params=pltpu.CompilerParams(
            has_side_effects=True, vmem_limit_bytes=40 * 1024 * 1024
        ),
        name="project",
    )(attn, weights)


def partial_attention(queries, key_cols, value_cols, allowed, inv_scale):
    scores = jnp.dot(queries, key_cols, preferred_element_type=jnp.float32) * inv_scale
    weights = jnp.where(allowed, jnp.exp(scores), jnp.float32(0.0))
    numerator = lax.dot_general(
        weights.astype(jnp.bfloat16),
        value_cols,
        (((1,), (1,)), ((), ())),
        preferred_element_type=jnp.float32,
    )
    return numerator, jnp.sum(weights, axis=1)


def body(
    qkv_master,
    adapter_down,
    adapter_up,
    adapter_pick,
    out_master,
    norm_gain,
    hidden_in,
    embed_in,
    prompt_len,
    prefix_len,
    prefix_holder,
    prefix_keys,
    prefix_values,
):
    chosen = adapter_pick[0]
    down_pick = lax.dynamic_index_in_dim(adapter_down, chosen, 0, keepdims=False)
    up_pick = lax.dynamic_index_in_dim(adapter_up, chosen, 0, keepdims=False).astype(jnp.bfloat16)
    joined = jnp.concatenate([hidden_in, embed_in], axis=1).astype(jnp.float32)
    factor = lax.rsqrt(jnp.mean(joined * joined, axis=1, keepdims=True) + 1e-05)
    normed = (joined * factor * norm_gain).astype(jnp.bfloat16)
    d_half = hidden_in.shape[1]

    sa, sb = pack(qkv_master, out_master, down_pick)
    ra, rb, xa, xb, gk, gv = exchange(
        sa, sb, normed[:, :d_half], normed[:, d_half:], prefix_keys[0].T, prefix_values[0].T
    )
    rows, cols = qkv_master.shape[0], up_pick.shape[1]
    out_rows = out_master.shape[0]
    head_size = cols // 3
    down_full = rb[:, :rows].reshape(128 * rows, -1)
    delta = jnp.dot(down_full, up_pick, preferred_element_type=jnp.float32)
    server_qkv = (ra.reshape(128 * rows, -1)[:, :cols].astype(jnp.float32) + delta).astype(
        jnp.bfloat16
    )
    server_out = jnp.concatenate(
        [rb[:, rows : rows + out_rows, :], ra[:, :out_rows, cols:]], axis=2
    ).reshape(128 * out_rows, head_size)
    all_rows = jnp.concatenate([xa.reshape(512, -1), xb.reshape(512, -1)], axis=1)
    qkv_rows = jnp.dot(all_rows, server_qkv, preferred_element_type=jnp.float32).astype(
        jnp.bfloat16
    )
    token_count = qkv_rows.shape[0]
    queries = qkv_rows[:, :head_size]
    new_keys = qkv_rows[:, head_size : 2 * head_size]
    new_values = qkv_rows[:, 2 * head_size :]
    inv_scale = 1.0 / math.sqrt(head_size)
    positions = jnp.arange(token_count, dtype=jnp.int32)
    lengths = prompt_len[0]
    request = (positions >= lengths[0]).astype(jnp.int32)
    allowed = (request[:, None] == request[None, :]) & (positions[None, :] <= positions[:, None])
    numerator, weight_sum = partial_attention(
        queries, new_keys.T, new_values.T, allowed, inv_scale
    )
    cached_len = prefix_len[0]
    holders = prefix_holder[0]
    slot_ids = jnp.arange(prefix_keys.shape[1], dtype=jnp.int32)
    for member in range(2):
        key_cols = lax.dynamic_index_in_dim(gk, holders[member], 0, keepdims=False)
        value_cols = lax.dynamic_index_in_dim(gv, holders[member], 0, keepdims=False)
        usable = (request == member)[:, None] & (slot_ids[None, :] < cached_len[member])
        part_num, part_sum = partial_attention(queries, key_cols, value_cols, usable, inv_scale)
        numerator = numerator + part_num
        weight_sum = weight_sum + part_sum
    attention = (numerator / weight_sum[:, None]).astype(jnp.bfloat16)
    block_out = project(attention, server_out)
    return (server_qkv, server_out, block_out, new_keys, new_values)


def solution(mesh):
    in_specs = (
        P(("dp", "tensor"), None),
        P(None, ("dp", "tensor"), None),
        P(None, None, "tensor"),
        P(),
        P(("dp", "tensor"), None),
        P(),
        P(("dp", "tensor"), None),
        P(("dp", "tensor"), None),
        P("dp", None),
        P("dp", None),
        P("dp", None),
        P("dp", None, "tensor"),
        P("dp", None, "tensor"),
    )
    out_specs = (
        P(None, "tensor"),
        P(None, "tensor"),
        P(("dp", "tensor"), None),
        P("dp", "tensor"),
        P("dp", "tensor"),
    )
    return jax.shard_map(body, mesh=mesh, in_specs=in_specs, out_specs=out_specs, check_vma=False)
```
